256 devices in a mesh: src: 128 (over x, z, y), lev: 2 (over core).
Axes of the slice: x: 4, y: 4, z: 8, core: 2. Of those that a mesh axis runs over, the one named last changes fastest.
Arguments:
- field: bfloat16 [262144, 256], P('src', 'lev'), may hold values from -6 to 6
- grad_coef: float32 [2, 4, 262144], P(None, None, 'src'), may hold values from -6 to 6
- neighbours: int32 [262144, 4], P('src'), may hold values from 0 to 2175, as said below
- level_weight: float32 [8], replicated, may hold values from 0.2 to 2
- src_index: int32 [16384, 64], P('src'), may hold values from 0 to 2047
- tgt_index: int32 [16384, 32], P('src'), may hold values from 0 to 1023
- block_dest: int32 [16384, 1], P('src'), may hold values from 0 to 127; in each aligned block of 128 rows (0 to 127, 128 to 255, ...) at most 2 rows name the same one
- weights: bfloat16 [16384, 6144], P('src'), may hold values from -0.21875 to 0.21875
Outputs:
- remapped: bfloat16 [131072, 256], P('src', 'lev')
- column_total: float32 [32, 131072], P(None, 'src')
The draws below stay inside these ranges and needn't reach their ends.
Inputs may be any that keep to these rules, and one draw needn't show every extreme that they name: `neighbours`: position 64 + p is the device's own cell p; positions below 64 and from 2112 on are the last and first cells of the devices before and after along the closed curve; a neighbour lies at most 64 cells from the cell. `block_dest`: the 128 blocks of one index of src name one target index at most 2 times.
All inputs are finite; a program needn't handle non-finite values.
Results may differ from the reference program's by a relative error of at most 0.0049.
Values may be sent and summed in bfloat16 or wider, within the bound.
No kernel may reach another device: no remote copies, remote signals or barrier semaphores. Data moves between devices by JAX's collectives and lax.ppermute only.
A program may use at most 128 MiB of HBM per device.

```python
import math
import jax
import jax.numpy as jnp
import numpy as np
from jax import lax

FIELDS = 32
LEVELS = 8
K = 4
HW = 64
SB = 64
TB = 32
S_DEV = 2048
T_DEV = 1024
B_DEV = 128
SOURCES = 262144
TARGETS = 131072
BLOCKS = 16384
CAP = 2
COLS = 256
N_SRC = 128


def draw_neighbours(key, part):
    offsets = jax.random.randint(key, (SOURCES, K), -HW, HW + 1)
    position = jnp.arange(SOURCES, dtype=jnp.int32) % S_DEV
    first_column = jnp.where(position == 0, -HW, offsets[:, 0])
    first_column = jnp.where(position == S_DEV - 1, HW, first_column)
    offsets = jnp.concatenate([first_column[:, None], offsets[:, 1:]], axis=1)
    return (position[:, None] + HW + offsets).astype(jnp.int32)


def set_ends(array, key, low, top_value):
    index_at = [jax.random.randint(jax.random.fold_in(key, axis), (), 0, length) for axis, length in enumerate(array.shape)]
    widest = array.shape.index(max(array.shape))
    neighbour = index_at[:widest] + [(index_at[widest] + 1) % array.shape[widest]] + index_at[widest + 1:]
    return array.at[tuple(index_at)].set(low).at[tuple(neighbour)].set(top_value)


def block_scale(stream_key, extent, pieces, least, top_value):
    level = 1.0
    for dim, parts in pieces:
        draws = jax.random.uniform(jax.random.fold_in(jax.random.fold_in(stream_key, 6), dim), (parts,), jnp.float32, least / len(pieces), top_value / len(pieces))
        level = level * jnp.repeat(jnp.exp(draws), extent[dim] // parts).reshape((-1,) + (1,) * (len(extent) - 1 - dim))
    return level


def routed_block(own_key, own, number, rows, amount, top, bound, skew):
    ranking = jax.random.permutation(own_key, amount)
    packed, common = shares(amount, rows * top, bound, skew, True), shares(amount, rows * top, bound, skew, False)
    places = jnp.arange(amount)

    def named(tallies, turn):
        used = int((tallies > 0).sum())
        fixed = max(1, used // 4)
        passed = fixed + (places - fixed + turn * (used - fixed)) % max(1, amount - fixed)
        return jnp.zeros((amount,), jnp.int32).at[ranking[jnp.where(places < fixed, places, passed)]].set(jnp.asarray(tallies, jnp.int32))

    tallies = jnp.where(number % 4 == 0, named(packed, number // 4), named(common, number - number // 4 - 1))
    mixed = jax.random.permutation(jax.random.fold_in(own, 3), amount)
    giver, taker = mixed[0:amount // 2 * 2:2], mixed[1:amount // 2 * 2:2]
    margin = jnp.minimum(tallies[giver] - 1, bound - tallies[taker]) // 2
    margin = jnp.where((giver == ranking[0]) | (taker == ranking[0]) | (tallies[taker] == 0), 0, jnp.maximum(margin, 0))
    passed = jax.random.randint(jax.random.fold_in(own, 4), (amount // 2,), 0, 1 << 20) % (margin + 1)
    tallies = tallies.at[giver].add(-passed).at[taker].add(passed)
    members = jnp.searchsorted(jnp.cumsum(tallies), jnp.arange(rows * top), side="right").astype(jnp.int32)
    table = members.reshape(top, rows).T
    table = table[jax.random.permutation(jax.random.fold_in(own, 1), rows)]
    turn = jax.random.randint(jax.random.fold_in(own, 2), (rows, 1), 0, top)
    return jnp.take_along_axis(table, (jnp.arange(top)[None, :] + turn) % top, axis=1)


def shares(number_of, total, limit, slope, full):
    weights = [(1 << 20) // math.isqrt(grade ** slope) + 1 for grade in range(1, number_of + 1)]
    largest = limit if full else min(limit, max(-(-total // number_of), total * weights[0] // sum(weights)))
    least = 1 if total - largest >= number_of - 1 else 0
    given, spare = [largest] + [least] * (number_of - 1), total - largest - least * (number_of - 1)
    while spare > 0:
        free = [i for i in range(1, number_of) if given[i] < largest] or [i for i in range(1, number_of) if given[i] < limit]
        mass, left = sum([weights[i] for i in free]), spare
        for i in free:
            addition = min(limit - given[i], max(1, left * weights[i] // mass), spare)
            given[i] = given[i] + addition
            spare = spare - addition
    return np.array(given)


def scatter_about(stream_key, shape, spread, limit, cuts=(), held_as=jnp.bfloat16):
    result = spread * jax.random.normal(stream_key, shape, jnp.float32)
    if cuts:
        result = result * block_scale(stream_key, shape, cuts, -0.22, 0.18)
    return jnp.clip(result, -limit, limit).astype(held_as)


def setup_inputs(seed: int = 0) -> dict:
    splits = jax.random.split(jax.random.key(seed), 9)
    field = scatter_about(splits[0], (SOURCES, COLS), 1.0, 6.0, ((0, 128), (1, 2)))
    grad_coef = scatter_about(splits[1], (2, K, SOURCES), 1.0, 6.0, ((2, 128),), jnp.float32)
    neighbours = draw_neighbours(jax.random.fold_in(splits[8], 71), 0)
    level_weight = jnp.clip(jnp.exp(jax.random.uniform(splits[3], (LEVELS,), jnp.float32, math.log(0.2), math.log(2.0))), 0.2, 2.0)
    src_index = set_ends(jax.random.randint(splits[4], (BLOCKS, SB), 0, S_DEV), jax.random.fold_in(splits[4], 1), 0, S_DEV - 1).astype(jnp.int32)
    tgt_index = set_ends(jax.random.randint(splits[5], (BLOCKS, TB), 0, T_DEV), jax.random.fold_in(splits[5], 1), 0, T_DEV - 1).astype(jnp.int32)
    block_dest_keys = jax.random.split(jax.random.fold_in(splits[6], 1), BLOCKS // B_DEV)
    block_dest_turns = jax.random.permutation(jax.random.fold_in(splits[6], 3), BLOCKS // B_DEV)
    block_dest = jax.vmap(lambda own, number: routed_block(jax.random.fold_in(splits[6], 2), own, number, B_DEV, N_SRC, 1, CAP, 2))(block_dest_keys, block_dest_turns).reshape((BLOCKS, 1))
    weights = scatter_about(splits[7], (BLOCKS, 3 * SB * TB), (12 * SB) ** -0.5, 0.21875, ((0, 128),))
    return {"field": field, "grad_coef": grad_coef, "neighbours": neighbours, "level_weight": level_weight, "src_index": src_index, "tgt_index": tgt_index, "block_dest": block_dest, "weights": weights}


def device_partial(extended, coefficients, neighbour_pos, source_cells, block_weights):
    own_values = extended[HW:HW + S_DEV]
    own_float = own_values.astype(jnp.float32)
    differ = extended[neighbour_pos].astype(jnp.float32) - own_float[:, None, :]
    grad_east = jnp.sum(coefficients[0].T[:, :, None] * differ, axis=1).astype(jnp.bfloat16)
    grad_north = jnp.sum(coefficients[1].T[:, :, None] * differ, axis=1).astype(jnp.bfloat16)
    recon = jnp.stack([own_values, grad_east, grad_north])
    picked = recon[:, source_cells]
    block_rows = jnp.transpose(picked, (1, 0, 2, 3)).reshape(source_cells.shape[0], 3 * SB, -1)
    shaped = block_weights.reshape(source_cells.shape[0], 3 * SB, TB)
    return jnp.einsum('bjt,bjc->btc', shaped.astype(jnp.float32), block_rows.astype(jnp.float32))


def reference(field, grad_coef, neighbours, level_weight, src_index, tgt_index, block_dest, weights):
    padded = jnp.concatenate([field[-HW:], field, field[:HW]], axis=0)
    coefficients = grad_coef.reshape(2, K, N_SRC, S_DEV).transpose(2, 0, 1, 3)
    neighbour_pos = neighbours.reshape(N_SRC, S_DEV, K)
    source_cells = src_index.reshape(N_SRC, B_DEV, SB)
    target_cells = ((block_dest[:, 0] * T_DEV)[:, None] + tgt_index).reshape(N_SRC, B_DEV * TB)
    block_weights = weights.reshape(N_SRC, B_DEV, 3 * SB * TB)

    def accumulate(total, inputs):
        device, coef_dev, nbr_dev, cells_dev, rows_dev, weights_dev = inputs
        extended = lax.dynamic_slice_in_dim(padded, device * S_DEV, S_DEV + 2 * HW, 0)
        partial_value = device_partial(extended, coef_dev, nbr_dev, cells_dev, weights_dev)
        return total.at[rows_dev].add(partial_value.reshape(-1, COLS)), None

    start = jnp.zeros((TARGETS, COLS), jnp.float32)
    devices = jnp.arange(N_SRC, dtype=jnp.int32)
    total, _ = lax.scan(accumulate, start, (devices, coefficients, neighbour_pos, source_cells, target_cells, block_weights))
    remapped = total.astype(jnp.bfloat16)
    column_total = jnp.einsum('tlf,l->ft', total.reshape(TARGETS, LEVELS, FIELDS), level_weight, precision=lax.Precision.HIGHEST)
    return remapped, column_total
```

```python
import jax
import jax.numpy as jnp
from jax import lax
from jax.experimental import pallas as pl
from jax.experimental.pallas import tpu as pltpu
from jax.sharding import PartitionSpec as P

FIELDS = 32
HW = 64
SB = 64
TB = 32
K = 4
S_DEV = 2048
T_DEV = 1024
B_DEV = 128
N_SRC = 128
COLS = 128
CAP = 2
TILE = 128
PITCH = 49
ROWS = 72
GROUP = 8
F32 = jnp.float32
BF16 = jnp.bfloat16

TN = (((0,), (0,)), ((), ()))
NN = (((1,), (0,)), ((), ()))
NT = (((1,), (1,)), ((), ()))


def source_kernel(
    src_ref,
    dest_ref,
    parity_ref,
    field_ref,
    low_ref,
    high_ref,
    coef_ref,
    nbr_ref,
    tgt_ref,
    w_ref,
    out_ref,
    ext,
    tab,
    wrows,
    xa,
    xb,
    cells,
    count,
):
    ext[0:HW, :] = low_ref[...]
    ext[HW : HW + S_DEV, :] = field_ref[...]
    ext[HW + S_DEV :, :] = high_ref[...]

    def spread(g, _):
        rows = w_ref[pl.ds(pl.multiple_of(g * 8, 8), 8), :].astype(F32)
        for q in range(48):
            wrows[pl.ds(g * (8 * PITCH) + q, 8, stride=PITCH), :] = rows[:, q * 128 : (q + 1) * 128]
        return 0

    lax.fori_loop(0, B_DEV // 8, spread, 0)

    position = lax.broadcasted_iota(jnp.int32, (2 * TILE, TILE), 0)
    lane = lax.broadcasted_iota(jnp.int32, (2 * TILE, TILE), 1)

    def gradients(t, _):
        p0 = pl.multiple_of(t * TILE, TILE)
        own = position == lane + HW
        near = nbr_ref[:, pl.ds(p0, TILE)] - p0
        east = jnp.zeros((2 * TILE, TILE), F32)
        north = jnp.zeros((2 * TILE, TILE), F32)
        for k in range(K):
            here = position == near[k : k + 1, :]
            east = east + jnp.where(here, coef_ref[0, k : k + 1, pl.ds(p0, TILE)], 0.0)
            north = north + jnp.where(here, coef_ref[1, k : k + 1, pl.ds(p0, TILE)], 0.0)
        sums = jnp.sum(coef_ref[:, :, pl.ds(p0, TILE)], axis=1)
        east = east - jnp.where(own, sums[0:1, :], 0.0)
        north = north - jnp.where(own, sums[1:2, :], 0.0)
        window = ext[pl.ds(p0, 2 * TILE), :]
        tab[pl.ds(p0 * 3, TILE, stride=3), :] = field_ref[pl.ds(p0, TILE), :].astype(F32)
        for c, full in ((1, east), (2, north)):
            top = full.astype(BF16)
            rest = (full - top.astype(F32)).astype(BF16)
            value = lax.dot_general(top, window, TN, preferred_element_type=F32)
            value = value + lax.dot_general(rest, window, TN, preferred_element_type=F32)
            tab[pl.ds(p0 * 3 + c, TILE, stride=3), :] = value.astype(BF16).astype(F32)
        return 0

    lax.fori_loop(0, S_DEV // TILE, gradients, 0)

    def clear(d, _):
        out_ref[d] = jnp.zeros((ROWS, COLS), BF16)
        cells[d] = jnp.zeros((8, 128), F32)
        count[d] = 0
        return 0

    lax.fori_loop(0, N_SRC, clear, 0)

    lanes = lax.broadcasted_iota(jnp.int32, (8, 128), 1) // TB
    sub = lax.broadcasted_iota(jnp.int32, (8, 128), 0)
    quarter = lax.broadcasted_iota(jnp.int32, (48, 128), 1) // TB
    parity = parity_ref[0]

    def gather(b, x):
        for j in range(SB):
            cell = src_ref[j, b]
            x[pl.ds((j % 4) * 48 + j // 4, 3, stride=16), :] = tab[pl.ds(cell * 3, 3), :]

    def product(b, x):
        chunk = wrows[pl.ds(b * PITCH, 48), :]
        spread_w = jnp.concatenate(
            [jnp.where(quarter == a, chunk, 0.0) for a in range(4)], axis=0
        ).astype(BF16)
        wide = lax.dot_general(spread_w, x[...].astype(BF16), TN, preferred_element_type=F32)
        part = wide[0:32] + wide[32:64] + wide[64:96] + wide[96:128]
        d = dest_ref[b, 0]
        rank = count[d]
        count[d] = rank + 1
        out_ref[d, pl.ds(pl.multiple_of(rank * TB, TB), TB), :] = part.astype(BF16)
        target = jnp.broadcast_to(tgt_ref[pl.ds(b, 1), :], (8, 128))
        pieces = jnp.where(sub == 0, target // 32, target % 32).astype(F32)
        mine = (lanes == parity * 2 + rank) & (sub < 2)
        cells[d] = jnp.where(mine, pieces, cells[d])

    gather(0, xa)

    def pair(i, _):
        b = i * 2
        gather(b + 1, xb)
        product(b, xa)
        gather(jnp.minimum(b + 2, B_DEV - 1), xa)
        product(b + 1, xb)
        return 0

    lax.fori_loop(0, B_DEV // 2, pair, 0)

    def finish(d, _):
        out_ref[d, CAP * TB : ROWS, :] = cells[d].astype(BF16)
        return 0

    lax.fori_loop(0, N_SRC, finish, 0)


def source_side(field, low, high, grad_coef, neighbours, src_index, tgt_index, block_dest, weights, parity):
    vmem = pl.BlockSpec(memory_space=pltpu.VMEM)
    smem = pl.BlockSpec(memory_space=pltpu.SMEM)
    return pl.pallas_call(
        source_kernel,
        out_shape=jax.ShapeDtypeStruct((N_SRC, ROWS, COLS), BF16),
        in_specs=[smem, smem, smem] + [vmem] * 7,
        out_specs=vmem,
        scratch_shapes=[
            pltpu.VMEM((S_DEV + 2 * HW, COLS), BF16),
            pltpu.VMEM((S_DEV * 3 + 8, COLS), F32),
            pltpu.VMEM((B_DEV * PITCH, 128), F32),
            pltpu.VMEM((3 * SB, COLS), F32),
            pltpu.VMEM((3 * SB, COLS), F32),
            pltpu.VMEM((N_SRC, 8, 128), F32),
            pltpu.SMEM((N_SRC,), jnp.int32),
        ],
        compiler_params=pltpu.CompilerParams(vmem_limit_bytes=48 << 20),
        name="source_side",
    )(
        src_index.T,
        block_dest,
        parity,
        field,
        low,
        high,
        grad_coef,
        neighbours.T,
        jnp.tile(tgt_index, (1, 4)),
        weights,
    )


def target_kernel(recv_ref, level_ref, out_ref, column_ref, acc):
    acc[...] = jnp.zeros_like(acc)
    low = lax.broadcasted_iota(jnp.int32, (32, 128), 0).astype(F32)

    def step(g, _):
        base = g * GROUP
        hot = []
        data = []
        for m in range(GROUP // 2):
            first, second = recv_ref[base + 2 * m], recv_ref[base + 2 * m + 1]
            data += [first[0 : CAP * TB], second[0 : CAP * TB]]
            cell = first[CAP * TB :].astype(F32) + second[CAP * TB :].astype(F32)
            top, bottom = cell[0:1, :], cell[1:2, :]
            inner = jnp.where(low == bottom, 1.0, 0.0).astype(BF16)
            hot.append(
                jnp.concatenate(
                    [jnp.where(jnp.broadcast_to(top, (32, 128)) == float(h), 1.0, 0.0).astype(BF16) * inner for h in range(32)],
                    axis=0,
                )
            )
        acc[...] += lax.dot_general(
            jnp.concatenate(hot, axis=1),
            jnp.concatenate(data, axis=0),
            NN,
            preferred_element_type=F32,
        )
        return 0

    lax.fori_loop(0, N_SRC // GROUP, step, 0)
    out_ref[...] = acc[...].astype(BF16)
    column_ref[...] = lax.dot_general(
        level_ref[...], acc[...], NT, preferred_element_type=F32, precision=lax.Precision.HIGHEST
    )


def target_side(recv, level_rows):
    vmem = pl.BlockSpec(memory_space=pltpu.VMEM)
    return pl.pallas_call(
        target_kernel,
        out_shape=(
            jax.ShapeDtypeStruct((T_DEV, COLS), BF16),
            jax.ShapeDtypeStruct((FIELDS, T_DEV), F32),
        ),
        in_specs=[vmem, vmem],
        out_specs=(vmem, vmem),
        scratch_shapes=[pltpu.VMEM((T_DEV, COLS), F32)],
        compiler_params=pltpu.CompilerParams(vmem_limit_bytes=48 << 20),
        name="target_side",
    )(recv, level_rows)


def shards(field, grad_coef, neighbours, level_weight, src_index, tgt_index, block_dest, weights):
    count = lax.axis_size("src")
    forward = [(i, (i + 1) % count) for i in range(count)]
    backward = [(t, s) for s, t in forward]
    low = lax.ppermute(field[S_DEV - HW :], "src", forward)
    high = lax.ppermute(field[:HW], "src", backward)
    parity = (lax.axis_index("src") % 2).reshape(1)
    send = source_side(
        field, low, high, grad_coef, neighbours, src_index, tgt_index, block_dest, weights, parity
    )
    recv = lax.all_to_all(send, "src", split_axis=0, concat_axis=0, tiled=True)
    levels = COLS // FIELDS
    share = lax.dynamic_slice_in_dim(level_weight, lax.axis_index("lev") * levels, levels)
    eye = jnp.eye(FIELDS, dtype=F32)
    level_rows = (eye[:, None, :] * share[None, :, None]).reshape(FIELDS, COLS)
    remapped, local_sum = target_side(recv, level_rows)
    other = lax.ppermute(local_sum, "lev", [(0, 1), (1, 0)])
    return remapped, local_sum + other


def solution(mesh):
    placed = (
        P("src", "lev"),
        P(None, None, "src"),
        P("src", None),
        P(),
        P("src", None),
        P("src", None),
        P("src", None),
        P("src", None),
    )
    return jax.shard_map(
        shards,
        mesh=mesh,
        in_specs=placed,
        out_specs=(P("src", "lev"), P(None, "src")),
        check_vma=False,
    )
```
